1024 devices in a mesh: seq: 16 (over y, x), frame: 64 (over z, core).
Axes of the slice: x: 4, y: 4, z: 32, core: 2. Of those that a mesh axis runs over, the one named last changes fastest.
Arguments:
- value_grad: bfloat16 [64, 16384, 512], P('frame', 'seq'), may hold values from -6 to 6
- w_value: bfloat16 [8192, 512], P('seq'), may hold values from -0.25 to 0.25
- norm_gain: float32 [8192], P('seq'), may hold values from 0.1 to 1.9
- vis_pos: int32 [64, 128], P('frame'), may hold values from 0 to 16383, as said below
- frame_owner: int32 [64, 128, 1], P('frame'), may hold values from 0 to 63; in each aligned block of 128 rows (0 to 127, 128 to 255, ..., all dimensions but the last counted through in order) at most 4 rows name the same one
- ques_span: int32 [64, 2], P('frame'), may hold values from 0 to 32, as said below
- vis_proj: bfloat16 [64, 128, 8192], P('frame', None, 'seq')
- vis_resid: bfloat16 [64, 128, 8192], P('frame', None, 'seq'), may hold values from -6 to 6
- ques_hidden: bfloat16 [64, 32, 8192], P('frame', None, 'seq'), may hold values from -6 to 6
- w_down: bfloat16 [8192, 8192], P(None, 'seq'), may hold values from -0.0625 to 0.0625
- pre_owned: bfloat16 [64, 8192, 256], P('frame', 'seq'), may hold values from -6 to 6
Outputs:
- pre_grad: bfloat16 [64, 8192, 256], P('frame', 'seq')
- ques_grad: bfloat16 [64, 32, 8192], P('frame', None, 'seq')
The draws below stay inside these ranges and needn't reach their ends.
Inputs may be any that keep to these rules, and one draw needn't show every extreme that they name: `vis_pos`: each row is distinct and increasing. `frame_owner`: in each sequence at most 4 visual tokens name the same owner. `ques_span`: column 1 is at least 1, and column 0 plus column 1 is at most 32.
All inputs are finite; a program needn't handle non-finite values.
Results may differ from the reference program's by a relative error of at most 0.015.
Values may be sent and summed in bfloat16 or wider, within the bound.
A program may use at most 64 MiB of HBM per device.

```python
import math
import jax
import jax.numpy as jnp
import numpy as np
from jax import lax

D = 8192
KV = 512
HID = 8192
NV = 128
QLEN = 32
SEQS = 64
SEQ_LEN = 16384
CAP = 4
SLOTS = 256
N_SEQ = 16
N_FRAME = 64


def draw_vis_pos(key, part):
    row_keys = jax.random.split(jax.random.fold_in(key, 11), SEQS)

    def one_row(row_key):
        return jnp.sort(jax.random.permutation(row_key, SEQ_LEN)[:NV]).astype(jnp.int32)
    return jax.vmap(one_row)(row_keys)


def draw_ques_span(key, part):
    first_key, second_key = jax.random.split(jax.random.fold_in(key, 23))
    lengths = jax.random.randint(first_key, (SEQS,), 1, QLEN + 1)
    lengths = lengths.at[0].set(QLEN)
    shifts = jax.random.randint(second_key, (SEQS,), 0, 1 << 20)
    starts = shifts % (QLEN - lengths + 1)
    return jnp.stack([starts, lengths], axis=1).astype(jnp.int32)


def draw_vis_proj(key, part):
    base_key, column_key, row_key = jax.random.split(jax.random.fold_in(key, 37), 3)
    column_pos = jnp.arange(D, dtype=jnp.float32) / (D - 1)
    column_scale = 3.0 ** column_pos * 3.0 ** jax.random.uniform(column_key, (D,), dtype=jnp.float32) / 3.0
    base = jax.random.normal(base_key, (SEQS, NV, D), dtype=jnp.float32)
    row_scale = 10.0 ** (jax.random.uniform(row_key, (SEQS, NV, 1), dtype=jnp.float32) - 0.5)
    return (base * column_scale[None, None, :] * row_scale).astype(jnp.bfloat16)


def levels(own_key, extent, shards, least, high):
    loudness, own = 1.0, jax.random.fold_in(own_key, 6)
    for dim, blocks in shards:
        steps = jnp.exp(jax.random.uniform(jax.random.fold_in(own, dim), (blocks,), jnp.float32, least / len(shards), high / len(shards)))
        loudness = loudness * jnp.repeat(steps, extent[dim] // blocks).reshape([-1 if axis == dim else 1 for axis in range(len(extent))])
    return loudness


def shared_out(key, own, number, rows, amount, top, most, skew):
    ranking = jax.random.permutation(key, amount)
    heavy_load, common = load_shares(amount, rows * top, most, skew, True), load_shares(amount, rows * top, most, skew, False)
    places = jnp.arange(amount)

    def named(sizes, offset_by):
        used = int((sizes > 0).sum())
        fixed = max(1, used // 4)
        moved = fixed + (places - fixed + offset_by * (used - fixed)) % max(1, amount - fixed)
        return jnp.zeros((amount,), jnp.int32).at[ranking[jnp.where(places < fixed, places, moved)]].set(jnp.asarray(sizes, jnp.int32))

    sizes = jnp.where(number % 4 == 0, named(heavy_load, number // 4), named(common, number - number // 4 - 1))
    mixed = jax.random.permutation(jax.random.fold_in(own, 3), amount)
    donor, receiver = mixed[0:amount // 2 * 2:2], mixed[1:amount // 2 * 2:2]
    slack = jnp.minimum(sizes[donor] - 1, most - sizes[receiver]) // 2
    slack = jnp.where((donor == ranking[0]) | (receiver == ranking[0]) | (sizes[receiver] == 0), 0, jnp.maximum(slack, 0))
    moved = jax.random.randint(jax.random.fold_in(own, 4), (amount // 2,), 0, 1 << 20) % (slack + 1)
    sizes = sizes.at[donor].add(-moved).at[receiver].add(moved)
    labels = jnp.searchsorted(jnp.cumsum(sizes), jnp.arange(rows * top), side="right").astype(jnp.int32)
    listing = labels.reshape(top, rows).T
    listing = listing[jax.random.permutation(jax.random.fold_in(own, 1), rows)]
    offset_by = jax.random.randint(jax.random.fold_in(own, 2), (rows, 1), 0, top)
    return jnp.take_along_axis(listing, (jnp.arange(top)[None, :] + offset_by) % top, axis=1)


def load_shares(count, total, bound, lean, full):
    portions = [(1 << 20) // math.isqrt(grade ** lean) + 1 for grade in range(1, count + 1)]
    largest = bound if full else min(bound, max(-(-total // count), total * portions[0] // sum(portions)))
    least = 1 if total - largest >= count - 1 else 0
    given, surplus = [largest] + [least] * (count - 1), total - largest - least * (count - 1)
    while surplus > 0:
        candidates = [i for i in range(1, count) if given[i] < largest] or [i for i in range(1, count) if given[i] < bound]
        mass, budget = sum([portions[i] for i in candidates]), surplus
        for i in candidates:
            more = min(bound - given[i], max(1, budget * portions[i] // mass), surplus)
            given[i] = given[i] + more
            surplus = surplus - more
    return np.array(given)


def bell_draw(key, shape, deviation, most, pieces=(), kind=jnp.bfloat16):
    result = jax.random.normal(key, shape, jnp.float32) * deviation
    if len(pieces) > 0:
        result = levels(key, shape, pieces, -0.22, 0.18) * result
    return jnp.clip(result, min=-most, max=most).astype(kind)


def setup_inputs(seed: int = 0) -> dict:
    seeds = jax.random.split(jax.random.key(seed), 12)
    value_grad = bell_draw(seeds[0], (SEQS, SEQ_LEN, KV), 1.0, 6.0, ((0, 64), (1, 16)))
    w_value = bell_draw(seeds[1], (D, KV), KV ** -0.5, 0.25, ((0, 16),))
    norm_gain = jnp.clip(1.0 + 0.18 * jax.random.normal(seeds[2], (D,), jnp.float32), 0.1, 1.9)
    vis_pos = draw_vis_pos(jax.random.fold_in(seeds[11], 71), 0)
    frame_owner_keys = jax.random.split(jax.random.fold_in(seeds[4], 1), SEQS * NV // NV)
    frame_owner_turns = jax.random.permutation(jax.random.fold_in(seeds[4], 3), SEQS * NV // NV)
    frame_owner = jax.vmap(lambda own, number: shared_out(jax.random.fold_in(seeds[4], 2), own, number, NV, N_FRAME, 1, CAP, 2))(frame_owner_keys, frame_owner_turns).reshape((SEQS, NV, 1))
    ques_span = draw_ques_span(jax.random.fold_in(seeds[11], 71), 0)
    vis_proj = draw_vis_proj(jax.random.fold_in(seeds[11], 71), 0)
    vis_resid = bell_draw(seeds[7], (SEQS, NV, D), 1.0, 6.0, ((0, 64), (2, 16)))
    ques_hidden = bell_draw(seeds[8], (SEQS, QLEN, D), 1.0, 6.0, ((0, 64), (2, 16)))
    w_down = bell_draw(seeds[9], (HID, D), D ** -0.5, 0.0625, ((1, 16),))
    pre_owned = bell_draw(seeds[10], (SEQS, HID, SLOTS), 1.0, 6.0, ((0, 64), (1, 16)))
    return {"value_grad": value_grad, "w_value": w_value, "norm_gain": norm_gain, "vis_pos": vis_pos, "frame_owner": frame_owner, "ques_span": ques_span, "vis_proj": vis_proj, "vis_resid": vis_resid, "ques_hidden": ques_hidden, "w_down": w_down, "pre_owned": pre_owned}


epsilon = 1e-06

def gelu_slope(pre_act):
    normal_cdf = 0.5 * (1.0 + lax.erf(pre_act * 0.7071067811865476))
    density = jnp.exp(-0.5 * pre_act * pre_act) * 0.3989422804014327
    return normal_cdf + pre_act * density

def reference(value_grad, w_value, norm_gain, vis_pos, frame_owner, ques_span, vis_proj, vis_resid, ques_hidden, w_down, pre_owned):
    picked = jnp.take_along_axis(value_grad, vis_pos.astype(jnp.int32)[:, :, None], axis=1)
    normed_grad = jnp.einsum('bjk,dk->bjd', picked.astype(jnp.float32), w_value.astype(jnp.float32))
    projected = vis_proj.astype(jnp.float32)
    residual = vis_resid.astype(jnp.float32)
    norm_scale = norm_gain.astype(jnp.float32)
    span_start = ques_span[:, 0]
    span_count = ques_span[:, 1]
    places = jnp.arange(QLEN, dtype=jnp.int32)
    span_mask = ((places[None, :] >= span_start[:, None]) & (places[None, :] < (span_start + span_count)[:, None])).astype(jnp.float32)
    count_value = span_count.astype(jnp.float32)
    quest_mean = jnp.einsum('bt,btd->bd', span_mask, ques_hidden.astype(jnp.float32)) / count_value[:, None]
    gate_scale = 4.0 / math.sqrt(D)
    sum_query = lax.optimization_barrier(jnp.sum(projected * quest_mean[:, None, :], axis=-1))
    sum_square = lax.optimization_barrier(jnp.sum(projected * projected, axis=-1))
    sum_norm = lax.optimization_barrier(jnp.sum(norm_scale * normed_grad * projected, axis=-1))
    sum_resid = lax.optimization_barrier(jnp.sum(residual * projected, axis=-1))
    gate_value = jax.nn.sigmoid(gate_scale * sum_query)
    inv_rms = lax.rsqrt(gate_value * gate_value * sum_square / D + epsilon)
    inner_sum = gate_value * sum_norm
    coef_value = gate_value * inv_rms * inv_rms * inv_rms * inner_sum / D
    input_grad = residual + inv_rms[..., None] * norm_scale * normed_grad - coef_value[..., None] * projected
    gate_grad = sum_resid + inv_rms * sum_norm - coef_value * sum_square
    logit_grad = gate_grad * gate_value * (1.0 - gate_value)
    proj_grad = (gate_value[..., None] * input_grad + (logit_grad * gate_scale)[..., None] * quest_mean[:, None, :]).astype(jnp.bfloat16)
    quest_grad = lax.optimization_barrier(jnp.sum((logit_grad * gate_scale)[..., None] * projected, axis=1))
    ques_out = (span_mask[:, :, None] * quest_grad[:, None, :] / count_value[:, None, None]).astype(jnp.bfloat16)
    owners = frame_owner[:, :, 0].astype(jnp.int32)
    owner_hot = (owners[:, :, None] == jnp.arange(N_FRAME, dtype=jnp.int32)[None, None, :]).astype(jnp.int32)
    earlier = jnp.cumsum(owner_hot, axis=1) - owner_hot
    rank_in_owner = lax.optimization_barrier(jnp.sum(earlier * owner_hot, axis=2))
    rank_hot = (rank_in_owner[:, :, None] == jnp.arange(CAP, dtype=jnp.int32)[None, None, :]).astype(jnp.float32)
    routed = jnp.einsum('bjo,bjc,bjd->obcd', owner_hot.astype(jnp.float32), rank_hot, proj_grad.astype(jnp.float32))
    routed = routed.reshape(N_FRAME, SEQS * CAP, D).astype(jnp.bfloat16)
    weight_split = w_down.astype(jnp.float32).reshape(HID, N_SEQ, D // N_SEQ)

    def owner_work(pairs):
        owner_rows, pre_slots = pairs
        rows_split = owner_rows.astype(jnp.float32).reshape(SEQS * CAP, N_SEQ, D // N_SEQ)
        partial_value = jnp.einsum('nsd,hsd->shn', rows_split, weight_split)
        rounded = lax.optimization_barrier(partial_value.astype(jnp.bfloat16))
        hidden_grad = lax.optimization_barrier(jnp.sum(rounded.astype(jnp.float32), axis=0))
        pre_act = pre_slots.astype(jnp.float32)
        return (hidden_grad * gelu_slope(pre_act)).astype(jnp.bfloat16)
    pre_out = lax.map(owner_work, (routed, pre_owned))
    return (pre_out, ques_out)
```

```python
import functools
import math

import jax
import jax.numpy as jnp
from jax import lax
from jax.experimental import pallas as pl
from jax.experimental.pallas import tpu as pltpu
from jax.sharding import PartitionSpec as P

MESH = pl.DeviceIdType.MESH
F32 = jnp.float32
BF16 = jnp.bfloat16
EPSILON = 1e-06
NT = (((1,), (1,)), ((), ()))
NN = (((1,), (0,)), ((), ()))
TN = (((0,), (0,)), ((), ()))


def mm(a, b, dims):
    return lax.dot_general(a, b, dims, preferred_element_type=F32)


def column(row):
    n = row.shape[1]
    return jnp.transpose(jnp.broadcast_to(row, (n, n)))


def gelu_slope(pre_act):
    normal_cdf = 0.5 * (1.0 + lax.erf(pre_act * 0.7071067811865476))
    density = jnp.exp(-0.5 * pre_act * pre_act) * 0.3989422804014327
    return normal_cdf + pre_act * density


def kernel(
    model_width,
    vg_any, wv_any, gain_ref, pos_ref, own_ref, span_ref, vp_any, vr_any, qh_any, wd_any, pre_any,
    out_ref, ques_ref,
    vg, wv, vp, vr, qh, wd, pre,
    snd1, sc1, r1, rs1, snd2, sc2, r2, rs2,
    h, relay1, stage1, near1, g1, relay2, stage2, near2, place, slope, snd3, r3,
    load_sem, ex_send, ex_recv, red_send, red_recv, z_send, z_recv, z_near,
):
    s = lax.axis_index("seq")
    f = lax.axis_index("frame")
    y, x = s // 4, s % 4
    z, core = f // 2, f % 2

    barrier = pltpu.get_barrier_semaphore()

    def greet(k, carry):
        pl.semaphore_signal(barrier, inc=1, device_id=(lax.rem(s + k, 16), f), device_id_type=MESH)
        return carry

    lax.fori_loop(1, 16, greet, 0)

    def z_device(step, other):
        return ((z + step + 32) % 32) * 2 + (core + other) % 2

    for step, other in ((0, 1), (1, 0), (1, 1), (-1, 0), (-1, 1)):
        pl.semaphore_signal(barrier, inc=1, device_id=(s, z_device(step, other)), device_id_type=MESH)

    loads = [
        pltpu.make_async_copy(src, dst, load_sem.at[i])
        for i, (src, dst) in enumerate(
            ((vg_any.at[0], vg), (vp_any.at[0], vp), (qh_any.at[0], qh), (vr_any.at[0], vr), (wv_any, wv), (pre_any.at[0], pre), (wd_any, wd))
        )
    ]
    for load in loads:
        load.start()
    load_vg, load_vp, load_qh, load_vr, load_wv, load_pre, load_wd = loads

    shard_len = vg.shape[0]
    tokens = vp.shape[0]
    lanes = lax.broadcasted_iota(jnp.int32, (tokens, 128), 1)

    place_of = column(pos_ref[...].astype(F32) - (s * shard_len).astype(F32))
    lane_value = lanes.astype(F32)
    select = jnp.concatenate(
        [(place_of == lane_value + float(128 * i)).astype(F32).astype(BF16) for i in range(shard_len // 128)], axis=1
    )
    load_vg.wait()
    own_rows = mm(select, vg[...], NN)

    load_qh.wait()
    count = span_ref[:, 1:2].astype(F32)
    start = span_ref[:, 0:1]
    rows32 = lax.broadcasted_iota(jnp.int32, (qh.shape[0], 1), 0)
    span_mask = ((rows32 >= start) & (rows32 < start + span_ref[:, 1:2])).astype(F32)
    quest_mean = jnp.sum(span_mask * qh[...].astype(F32), axis=0, keepdims=True) / count
    load_vp.wait()
    projected = vp[...].astype(F32)
    gain = gain_ref[...]
    scaled = gain * projected
    scaled_hi = scaled.astype(BF16)
    scaled_lo = (scaled - scaled_hi.astype(F32)).astype(BF16)
    load_wv.wait()
    mixed = mm(scaled_hi, wv[...], NN) + mm(scaled_lo, wv[...], NN)
    sum_query = jnp.sum(projected * quest_mean, axis=1, keepdims=True)
    sum_square = jnp.sum(projected * projected, axis=1, keepdims=True)
    load_vr.wait()
    sum_resid = jnp.sum(vr[...].astype(F32) * projected, axis=1, keepdims=True)
    sums = jnp.where(lanes == 0, sum_query, jnp.where(lanes == 1, sum_square, jnp.where(lanes == 2, sum_resid, 0.0)))
    width = own_rows.shape[1]
    snd1[...] = jnp.concatenate([own_rows.reshape(16, 8, width), mixed.reshape(16, 8, width)], axis=1).astype(BF16)
    sc1[...] = sums.reshape(16, 8, 128)

    pl.semaphore_wait(barrier, 20)

    def send1(k, carry):
        t = lax.rem(s + k, 16)
        pltpu.make_async_remote_copy(
            src_ref=snd1.at[t], dst_ref=r1.at[s], send_sem=ex_send.at[0], recv_sem=ex_recv.at[0], device_id=(t, f), device_id_type=MESH
        ).start()
        pltpu.make_async_remote_copy(
            src_ref=sc1.at[t], dst_ref=rs1.at[s], send_sem=ex_send.at[1], recv_sem=ex_recv.at[1], device_id=(t, f), device_id_type=MESH
        ).start()
        return carry

    lax.fori_loop(1, 16, send1, 0)
    r1[pl.ds(s, 1)] = snd1[pl.ds(s, 1)]
    rs1[pl.ds(s, 1)] = sc1[pl.ds(s, 1)]

    def z_tell(level):
        for step in (1 << level, -(1 << level)):
            pl.semaphore_signal(z_near.at[level], inc=1, device_id=(s, z_device(step, 0)), device_id_type=MESH)

    z_tell(0)
    owner = own_ref[...]
    owner_value = owner.astype(F32)
    same = (column(owner_value) == owner_value) & (lax.broadcasted_iota(jnp.int32, (tokens, tokens), 0) < lanes)
    rank = jnp.sum(same.astype(F32), axis=0, keepdims=True)
    target = owner_value * 4.0 + rank
    rows = place.shape[0]
    target2 = jnp.concatenate([target, target], axis=1)
    row_id = lax.broadcasted_iota(jnp.int32, (rows, 1), 0)
    slot_of_row = ((row_id >> 3) * 4 + (row_id & 3)).astype(F32)
    half_of_row = (row_id >> 2) & 1
    lane_half = lax.broadcasted_iota(jnp.int32, (1, 2 * tokens), 1) >> 7
    place[...] = ((target2 == slot_of_row) & (half_of_row == lane_half)).astype(F32).astype(BF16)
    pl.semaphore_wait(z_near.at[0], 2)
    z_tell(1)
    load_pre.wait()
    slope[...] = gelu_slope(pre[...].astype(F32))
    pl.semaphore_wait(z_near.at[1], 2)
    z_tell(2)

    def wait_all(buffer, amount, sems, i):
        view = buffer.at[pl.ds(0, amount)]
        pltpu.make_async_copy(view, view, sems.at[i]).wait()

    wait_all(r1, 15, ex_recv, 0)
    wait_all(rs1, 15, ex_recv, 1)
    total = r1[0].astype(F32)
    sums = rs1[0]
    for i in range(1, 16):
        total = total + r1[i].astype(F32)
        sums = sums + rs1[i]
    picked8 = total[0:8]
    sum_norm = jnp.sum(picked8 * total[8:16], axis=1, keepdims=True)
    sum_query, sum_square, sum_resid = sums[:, 0:1], sums[:, 1:2], sums[:, 2:3]
    gate_scale = 4.0 / math.sqrt(model_width)
    gate = jax.nn.sigmoid(gate_scale * sum_query)
    inv_rms = lax.rsqrt(gate * gate * sum_square / model_width + EPSILON)
    coef = gate * inv_rms * inv_rms * inv_rms * (gate * sum_norm) / model_width
    gate_grad = sum_resid + inv_rms * sum_norm - coef * sum_square
    logit = gate_grad * gate * (1.0 - gate) * gate_scale
    lanes8 = lanes[0:8]
    sc2[...] = jnp.where(
        lanes8 == 0, gate, jnp.where(lanes8 == 1, inv_rms, jnp.where(lanes8 == 2, coef, jnp.where(lanes8 == 3, logit, 0.0)))
    )
    snd2[...] = picked8.astype(BF16)

    def send2(k, carry):
        t = lax.rem(s + k, 16)
        pltpu.make_async_remote_copy(
            src_ref=snd2, dst_ref=r2.at[s], send_sem=ex_send.at[2], recv_sem=ex_recv.at[2], device_id=(t, f), device_id_type=MESH
        ).start()
        pltpu.make_async_remote_copy(
            src_ref=sc2, dst_ref=rs2.at[s], send_sem=ex_send.at[3], recv_sem=ex_recv.at[3], device_id=(t, f), device_id_type=MESH
        ).start()
        return carry

    lax.fori_loop(1, 16, send2, 0)
    r2[pl.ds(s, 1)] = snd2[...][None]
    rs2[pl.ds(s, 1)] = sc2[...][None]
    pl.semaphore_wait(z_near.at[2], 2)
    z_tell(3)
    load_wd.wait()
    wait_all(r2, 15, ex_recv, 2)
    wait_all(rs2, 15, ex_recv, 3)

    picked = r2[...].astype(F32).reshape(tokens, width).astype(BF16)
    scalars = rs2[...].reshape(tokens, 128)
    normed_grad = mm(picked, wv[...], NT)
    projected = vp[...].astype(F32)
    logit_all = scalars[:, 3:4]
    input_grad = vr[...].astype(F32) + scalars[:, 1:2] * gain * normed_grad - scalars[:, 2:3] * projected
    proj_grad = (scalars[:, 0:1] * input_grad + logit_all * quest_mean).astype(BF16)

    def hop(half, second, step):
        if (half == 0) != second:
            return y * 4 + (x + step + 4) % 4, f
        return ((y + step + 4) % 4) * 4 + x, f

    def at(half, second, step):
        coord = x if (half == 0) != second else y
        return (coord + step + 4) % 4

    def products(half, c, step):
        major = at(half, False, step)
        blocks = []
        for minor in range(4):
            block = (minor * 4 + major) if half == 0 else (major * 4 + minor)
            blocks.append(wd[pl.ds(pl.multiple_of(block * 512 + half * 256 + c * 128, 128), 128), :])
        h[half, c, major] = mm(jnp.concatenate(blocks, axis=0), proj_grad, NT).astype(BF16)

    started = []

    def ship(src, dst, second, half, c, which, step):
        copy = pltpu.make_async_remote_copy(
            src_ref=src, dst_ref=dst, send_sem=red_send.at[int(second), half, c, which], recv_sem=red_recv.at[int(second), half, c, which],
            device_id=hop(half, second, step), device_id_type=MESH,
        )
        copy.start()
        started.append(copy)
        return copy

    copies = {}

    def first_sends(second, half, c):
        if second:
            size = 64
            part = lambda step, low: g1.at[half, c, pl.ds(at(half, True, step) * 128 + low * size, size)]
            relay, near = relay2, near2
        else:
            size = 256
            part = lambda step, low: h.at[half, c, at(half, False, step), pl.ds(low * size, size)]
            relay, near = relay1, near1
        copies[second, half, c, 0] = ship(part(2, 0), relay.at[half, c, 0], second, half, c, 0, 1)
        copies[second, half, c, 1] = ship(part(2, 1), relay.at[half, c, 1], second, half, c, 1, -1)
        copies[second, half, c, 2] = ship(part(1, 1), near.at[half, c, 0, pl.ds(size, size)], second, half, c, 2, 1)
        copies[second, half, c, 3] = ship(part(-1, 0), near.at[half, c, 1, pl.ds(0, size)], second, half, c, 3, -1)

    def second_sends(second, half, c):
        if second:
            size = 64
            own = lambda step, low: g1[half, c, pl.ds(at(half, True, step) * 128 + low * size, size)]
            relay, near, stage = relay2, near2, stage2
        else:
            size = 256
            own = lambda step, low: h[half, c, at(half, False, step), low * size:(low + 1) * size]
            relay, near, stage = relay1, near1, stage1
        for i, step in ((0, 1), (1, -1)):
            copies[second, half, c, i].wait_recv()
            stage[half, c, i] = (own(step, i).astype(F32) + relay[half, c, i].astype(F32)).astype(BF16)
            copies[second, half, c, 4 + i] = ship(
                stage.at[half, c, i], near.at[half, c, i, pl.ds(i * size, size)], second, half, c, 4 + i, step
            )

    def collect(second, half, c):
        for which in (2, 3, 4, 5):
            copies[second, half, c, which].wait_recv()
        if second:
            mine = g1[half, c, pl.ds(at(half, True, 0) * 128, 128)]
            return mine.astype(F32) + near2[half, c, 0].astype(F32) + near2[half, c, 1].astype(F32)
        mine = h[half, c, at(half, False, 0)]
        return mine.astype(F32) + near1[half, c, 0].astype(F32) + near1[half, c, 1].astype(F32)

    def z_target(k):
        far = jnp.where(k < 2, 16, 15 - (k - 2) // 4)
        sign = jnp.where(k < 2, 1, jnp.where(((k - 2) // 2) % 2 == 0, 1, -1))
        target = ((z + sign * far + 64) % 32) * 2 + (core + k) % 2
        return jnp.where(k == 62, z * 2 + (1 - core), target)

    def route(c):
        both = jnp.concatenate([collect(True, 0, c), collect(True, 1, c)], axis=1).astype(BF16)
        snd3[c] = mm(place[...], both, NT).reshape(64, 8, 128).astype(BF16)

        def send3(k, carry):
            t = z_target(k)
            pltpu.make_async_remote_copy(
                src_ref=snd3.at[c, t], dst_ref=r3.at[c, f], send_sem=z_send.at[c], recv_sem=z_recv.at[c], device_id=(s, t), device_id_type=MESH
            ).start()
            return carry

        lax.fori_loop(0, 63, send3, 0)
        r3[c, pl.ds(f, 1)] = snd3[c, pl.ds(f, 1)]

    halves = (0, 1)
    for half in halves:
        products(half, 0, 2)
    for half in halves:
        products(half, 0, 1)
        products(half, 0, -1)
        first_sends(False, half, 0)
    for half in halves:
        products(half, 0, 0)
        products(half, 1, 2)
        products(half, 1, 1)
        products(half, 1, -1)
    for half in halves:
        second_sends(False, half, 0)
        first_sends(False, half, 1)
    for half in halves:
        products(half, 1, 0)
    ques_row = jnp.sum(logit_all * projected, axis=0, keepdims=True)
    ques_ref[0] = (span_mask * ques_row / count).astype(BF16)
    for half in halves:
        g1[half, 0] = collect(False, half, 0).astype(BF16)
        first_sends(True, half, 0)
    for half in halves:
        second_sends(False, half, 1)
    for half in halves:
        second_sends(True, half, 0)
    pl.semaphore_wait(z_near.at[3], 2)
    route(0)
    for half in halves:
        g1[half, 1] = collect(False, half, 1).astype(BF16)
        first_sends(True, half, 1)
    for half in halves:
        second_sends(True, half, 1)
    route(1)

    slots = out_ref.shape[2]
    row_id = lax.broadcasted_iota(jnp.int32, (rows, slots), 0)
    slot_id = lax.broadcasted_iota(jnp.int32, (rows, slots), 1)
    meets = (row_id >> 3) * 4 + (row_id & 3) == slot_id
    takes = [(meets & (((row_id >> 2) & 1) == half)).astype(F32).astype(BF16) for half in halves]
    for c in range(2):
        view = r3.at[c, pl.ds(0, 63)]
        pltpu.make_async_copy(view, view, z_recv.at[c]).wait()
        arrived = r3[c].astype(F32).reshape(rows, 128).astype(BF16)
        for half in halves:
            at_rows = slice(half * 256 + c * 128, half * 256 + c * 128 + 128)
            out_ref[0, at_rows] = (mm(arrived, takes[half], TN) * slope[at_rows]).astype(BF16)

    for c in range(2):
        view = r3.at[c, pl.ds(0, 63)]
        pltpu.make_async_copy(view, view, z_send.at[c]).wait()
    for copy in started:
        copy.wait_send()
    wait_all(r1, 15, ex_send, 0)
    wait_all(rs1, 15, ex_send, 1)
    wait_all(r2, 15, ex_send, 2)
    wait_all(rs2, 15, ex_send, 3)


def solution(mesh):
    def body(value_grad, w_value, norm_gain, vis_pos, frame_owner, ques_span, vis_proj, vis_resid, ques_hidden, w_down, pre_owned):
        model_width = vis_proj.shape[2] * mesh.shape["seq"]
        in_vmem = pl.BlockSpec(memory_space=pltpu.VMEM)
        in_any = pl.BlockSpec(memory_space=pl.ANY)
        dma = pltpu.SemaphoreType.DMA
        return pl.pallas_call(
            functools.partial(kernel, model_width),
            out_shape=(
                jax.ShapeDtypeStruct(pre_owned.shape, BF16),
                jax.ShapeDtypeStruct(ques_hidden.shape, BF16),
            ),
            in_specs=[in_any, in_any, in_vmem, in_vmem, in_vmem, in_vmem, in_any, in_any, in_any, in_any, in_any],
            out_specs=(in_vmem, in_vmem),
            scratch_shapes=[
                pltpu.VMEM((1024, 512), BF16),
                pltpu.VMEM((512, 512), BF16),
                pltpu.VMEM((128, 512), BF16),
                pltpu.VMEM((128, 512), BF16),
                pltpu.VMEM((32, 512), BF16),
                pltpu.VMEM((8192, 512), BF16),
                pltpu.VMEM((512, 256), BF16),
                pltpu.VMEM((16, 16, 512), BF16),
                pltpu.VMEM((16, 8, 128), F32),
                pltpu.VMEM((16, 16, 512), BF16),
                pltpu.VMEM((16, 8, 128), F32),
                pltpu.VMEM((8, 512), BF16),
                pltpu.VMEM((8, 128), F32),
                pltpu.VMEM((16, 8, 512), BF16),
                pltpu.VMEM((16, 8, 128), F32),
                pltpu.VMEM((2, 2, 4, 512, 128), BF16),
                pltpu.VMEM((2, 2, 2, 256, 128), BF16),
                pltpu.VMEM((2, 2, 2, 256, 128), BF16),
                pltpu.VMEM((2, 2, 2, 512, 128), BF16),
                pltpu.VMEM((2, 2, 512, 128), BF16),
                pltpu.VMEM((2, 2, 2, 64, 128), BF16),
                pltpu.VMEM((2, 2, 2, 64, 128), BF16),
                pltpu.VMEM((2, 2, 2, 128, 128), BF16),
                pltpu.VMEM((512, 256), BF16),
                pltpu.VMEM((512, 256), F32),
                pltpu.VMEM((2, 64, 8, 128), BF16),
                pltpu.VMEM((2, 64, 8, 128), BF16),
                dma((7,)),
                dma((4,)),
                dma((4,)),
                dma((2, 2, 2, 6)),
                dma((2, 2, 2, 6)),
                dma((2,)),
                dma((2,)),
                pltpu.SemaphoreType.REGULAR((4,)),
            ],
            compiler_params=pltpu.CompilerParams(collective_id=0, has_side_effects=True, vmem_limit_bytes=56 * 1024 * 1024),
        )(
            value_grad,
            w_value,
            norm_gain.reshape(1, -1),
            vis_pos,
            frame_owner.reshape(1, -1),
            ques_span,
            vis_proj,
            vis_resid,
            ques_hidden,
            w_down,
            pre_owned,
        )

    in_specs = (
        P("frame", "seq", None),
        P("seq", None),
        P("seq"),
        P("frame", None),
        P("frame", None, None),
        P("frame", None),
        P("frame", None, "seq"),
        P("frame", None, "seq"),
        P("frame", None, "seq"),
        P(None, "seq"),
        P("frame", "seq", None),
    )
    out_specs = (P("frame", "seq", None), P("frame", None, "seq"))
    return jax.shard_map(body, mesh=mesh, in_specs=in_specs, out_specs=out_specs, check_vma=False)
```

```python
import functools
import math

import jax
import jax.numpy as jnp
from jax import lax
from jax.experimental import pallas as pl
from jax.experimental.pallas import tpu as pltpu
from jax.sharding import PartitionSpec as P

MESH = pl.DeviceIdType.MESH
F32 = jnp.float32
BF16 = jnp.bfloat16
EPSILON = 1e-06
NT = (((1,), (1,)), ((), ()))
NN = (((1,), (0,)), ((), ()))
TN = (((0,), (0,)), ((), ()))


def mm(a, b, dims):
    return lax.dot_general(a, b, dims, preferred_element_type=F32)


def column(row):
    n = row.shape[1]
    return jnp.transpose(jnp.broadcast_to(row, (n, n)))


def triple(values):
    high = values.astype(BF16).astype(F32)
    rest = values - high
    middle = rest.astype(BF16).astype(F32)
    low = (rest - middle).astype(BF16).astype(F32)
    return high + pltpu.roll(middle, 8, 1) + pltpu.roll(low, 16, 1)


def untriple(terms):
    return terms[:, 0:8] + terms[:, 8:16] + terms[:, 16:24]


def gelu_slope(pre_act):
    normal_cdf = 0.5 * (1.0 + lax.erf(pre_act * 0.7071067811865476))
    density = jnp.exp(-0.5 * pre_act * pre_act) * 0.3989422804014327
    return normal_cdf + pre_act * density


def kernel(
    model_width,
    vg_any, wv_any, gain_any, pos_any, own_any, span_any, vp_any, vr_any, qh_any, wd_any, pre_any,
    out_ref, ques_ref,
    vg, wv, gain_ref, pos_ref, own_ref, span_ref, vp, vr, qh, wd, pre,
    snd1, r1, snd2, r2,
    h, relay1, stage1, near1, g1, near2, place, slope, snd3, r3,
    load_sem, ex_send, ex_recv, red_send, red_recv, z_send, z_recv, z_near,
):
    s = lax.axis_index("seq")
    f = lax.axis_index("frame")
    y, x = s // 4, s % 4
    z, core = f // 2, f % 2

    ys = [y] + [(y + step) % 4 for step in (1, 2, 3)]
    xs = [x] + [(x + step) % 4 for step in (1, 2, 3)]
    hops = (0, 1, 2, 1)
    offsets = sorted(((i, j) for i in range(4) for j in range(4) if i or j), key=lambda o: -hops[o[0]] - hops[o[1]])
    others = [ys[i] * 4 + xs[j] for i, j in offsets]

    copies_in = [
        pltpu.make_async_copy(src, dst, load_sem.at[i])
        for i, (src, dst) in enumerate(
            (
                (pos_any, pos_ref), (vg_any.at[0], vg), (qh_any.at[0], qh), (span_any, span_ref), (vp_any.at[0], vp), (gain_any, gain_ref),
                (wv_any, wv), (vr_any.at[0], vr), (own_any, own_ref), (pre_any.at[0], pre), (wd_any, wd),
            )
        )
    ]
    load_pos, load_vg, load_qh, load_span, load_vp, load_gain, load_wv, load_vr, load_own, load_pre, load_wd = copies_in
    load_pos.start()
    load_vg.start()

    barrier = pltpu.get_barrier_semaphore()
    for t in others:
        pl.semaphore_signal(barrier, inc=1, device_id=(t, f), device_id_type=MESH)

    def z_device(step, other):
        return ((z + step + 32) % 32) * 2 + (core + other) % 2

    for step, other in ((1, 0), (1, 1), (-1, 0), (-1, 1), (0, 1)):
        pl.semaphore_signal(barrier, inc=1, device_id=(s, z_device(step, other)), device_id_type=MESH)
    for load in copies_in[2:]:
        load.start()

    shard_len = vg.shape[0]
    tokens = vp.shape[0]
    lanes = lax.broadcasted_iota(jnp.int32, (tokens, 128), 1)

    load_pos.wait()
    place_of = column(pos_ref[...].astype(F32) - (s * shard_len).astype(F32))
    lane_value = lanes.astype(F32)
    select = jnp.concatenate(
        [(place_of == lane_value + float(128 * i)).astype(F32).astype(BF16) for i in range(shard_len // 128)], axis=1
    )
    load_vg.wait()
    own_rows = mm(select, vg[...], NN)

    load_qh.wait()
    load_span.wait()
    count = span_ref[:, 1:2].astype(F32)
    start = span_ref[:, 0:1]
    rows32 = lax.broadcasted_iota(jnp.int32, (qh.shape[0], 1), 0)
    span_mask = ((rows32 >= start) & (rows32 < start + span_ref[:, 1:2])).astype(F32)
    quest_mean = jnp.sum(span_mask * qh[...].astype(F32), axis=0, keepdims=True) / count
    load_vp.wait()
    projected = vp[...].astype(F32)
    load_gain.wait()
    gain = gain_ref[...]
    scaled = gain * projected
    scaled_hi = scaled.astype(BF16)
    scaled_lo = (scaled - scaled_hi.astype(F32)).astype(BF16)
    load_wv.wait()
    mixed = mm(scaled_hi, wv[...], NN) + mm(scaled_lo, wv[...], NN)
    sum_query = jnp.sum(projected * quest_mean, axis=1, keepdims=True)
    sum_square = jnp.sum(projected * projected, axis=1, keepdims=True)
    load_vr.wait()
    sum_resid = jnp.sum(vr[...].astype(F32) * projected, axis=1, keepdims=True)
    sums = jnp.where(lanes == 0, sum_query, jnp.where(lanes == 1, sum_square, jnp.where(lanes == 2, sum_resid, 0.0)))
    width = own_rows.shape[1]
    for at_rows, part in ((slice(0, 8), own_rows), (slice(8, 16), mixed)):
        snd1[:, at_rows, 0:width] = part.reshape(16, 8, width).astype(BF16)
    snd1[:, 0:8, width:] = triple(sums).reshape(16, 8, 128).astype(BF16)
    snd1[:, 8:16, width:] = jnp.zeros((16, 8, 128), BF16)

    pl.semaphore_wait(barrier, 20)

    def exchange(source, buffer, i):
        for t in others:
            pltpu.make_async_remote_copy(
                src_ref=source(t), dst_ref=buffer.at[s], send_sem=ex_send.at[i], recv_sem=ex_recv.at[i], device_id=(t, f), device_id_type=MESH
            ).start()

    exchange(lambda t: snd1.at[t], r1, 0)
    r1[pl.ds(s, 1)] = snd1[pl.ds(s, 1)]

    def z_tell(level):
        for step in (1 << level, -(1 << level)):
            pl.semaphore_signal(z_near.at[level], inc=1, device_id=(s, z_device(step, 0)), device_id_type=MESH)

    z_tell(0)
    load_own.wait()
    owner = own_ref[...]
    owner_value = owner.astype(F32)
    same = (column(owner_value) == owner_value) & (lax.broadcasted_iota(jnp.int32, (tokens, tokens), 0) < lanes)
    rank = jnp.sum(same.astype(F32), axis=0, keepdims=True)
    target = owner_value * 4.0 + rank
    rows = place.shape[0]
    target2 = jnp.concatenate([target, target], axis=1)
    row_id = lax.broadcasted_iota(jnp.int32, (rows, 1), 0)
    slot_of_row = ((row_id >> 3) * 4 + (row_id & 3)).astype(F32)
    half_of_row = (row_id >> 2) & 1
    lane_half = lax.broadcasted_iota(jnp.int32, (1, 2 * tokens), 1) >> 7
    place[...] = ((target2 == slot_of_row) & (half_of_row == lane_half)).astype(F32).astype(BF16)
    pl.semaphore_wait(z_near.at[0], 2)
    z_tell(1)
    load_pre.wait()
    slope[...] = gelu_slope(pre[...].astype(F32))
    pl.semaphore_wait(z_near.at[1], 2)
    z_tell(2)

    def wait_all(buffer, amount, sems, i):
        view = buffer.at[pl.ds(0, amount)]
        pltpu.make_async_copy(view, view, sems.at[i]).wait()

    wait_all(r1, 15, ex_recv, 0)
    total = r1[0].astype(F32)
    for i in range(1, 16):
        total = total + r1[i].astype(F32)
    picked8 = total[0:8, 0:width]
    sum_norm = jnp.sum(picked8 * total[8:16, 0:width], axis=1, keepdims=True)
    sums = untriple(total[0:8, width:])
    sum_query, sum_square, sum_resid = sums[:, 0:1], sums[:, 1:2], sums[:, 2:3]
    gate_scale = 4.0 / math.sqrt(model_width)
    gate = jax.nn.sigmoid(gate_scale * sum_query)
    inv_rms = lax.rsqrt(gate * gate * sum_square / model_width + EPSILON)
    coef = gate * inv_rms * inv_rms * inv_rms * (gate * sum_norm) / model_width
    gate_grad = sum_resid + inv_rms * sum_norm - coef * sum_square
    logit = gate_grad * gate * (1.0 - gate) * gate_scale
    lanes8 = lanes[0:8]
    scalars = jnp.where(
        lanes8 == 0, gate, jnp.where(lanes8 == 1, inv_rms, jnp.where(lanes8 == 2, coef, jnp.where(lanes8 == 3, logit, 0.0)))
    )
    snd2[:, 0:width] = picked8.astype(BF16)
    snd2[:, width:] = triple(scalars).astype(BF16)
    exchange(lambda t: snd2, r2, 1)
    r2[pl.ds(s, 1)] = snd2[...][None]
    pl.semaphore_wait(z_near.at[2], 2)
    z_tell(3)
    load_wd.wait()
    wait_all(r2, 15, ex_recv, 1)

    gathered = r2[...].astype(F32).reshape(tokens, width + 128)
    picked = gathered[:, 0:width].astype(BF16)
    scalars = untriple(gathered[:, width:])
    normed_grad = mm(picked, wv[...], NT)
    projected = vp[...].astype(F32)
    logit_all = scalars[:, 3:4]
    input_grad = vr[...].astype(F32) + scalars[:, 1:2] * gain * normed_grad - scalars[:, 2:3] * projected
    proj_grad = (scalars[:, 0:1] * input_grad + logit_all * quest_mean).astype(BF16)

    def hop(half, second, step):
        if (half == 0) != second:
            return y * 4 + (x + step + 4) % 4, f
        return ((y + step + 4) % 4) * 4 + x, f

    def at(half, second, step):
        coord = x if (half == 0) != second else y
        return (coord + step + 4) % 4

    def products(half, c, step):
        major = at(half, False, step)
        blocks = []
        for minor in range(4):
            block = (minor * 4 + major) if half == 0 else (major * 4 + minor)
            blocks.append(wd[pl.ds(pl.multiple_of(block * 512 + half * 256 + c * 128, 128), 128), :])
        h[half, c, major] = mm(jnp.concatenate(blocks, axis=0), proj_grad, NT).astype(BF16)

    def ship(src, dst, second, half, c, which, step):
        copy = pltpu.make_async_remote_copy(
            src_ref=src, dst_ref=dst, send_sem=red_send.at[int(second)], recv_sem=red_recv.at[half, c, which],
            device_id=hop(half, second, step), device_id_type=MESH,
        )
        copy.start()
        return copy

    copies = {}

    def first_sends(half, c, whiches):
        def part(step, low):
            return h.at[half, c, at(half, False, step), pl.ds(low * 256, 256)]

        plan = (
            (part(2, 0), relay1.at[half, c, 0], 1),
            (part(2, 1), relay1.at[half, c, 1], -1),
            (part(1, 1), near1.at[half, c, 0, pl.ds(256, 256)], 1),
            (part(-1, 0), near1.at[half, c, 1, pl.ds(0, 256)], -1),
        )
        for which in whiches:
            src, dst, way = plan[which]
            copies[half, c, which] = ship(src, dst, False, half, c, which, way)

    def relayed_sends(half, c):
        for i, step in ((0, 1), (1, -1)):
            copies[half, c, i].wait_recv()
            own = h[half, c, at(half, False, step), i * 256:(i + 1) * 256]
            stage1[half, c, i] = (own.astype(F32) + relay1[half, c, i].astype(F32)).astype(BF16)
            copies[half, c, 4 + i] = ship(
                stage1.at[half, c, i], near1.at[half, c, i, pl.ds(i * 256, 256)], False, half, c, 4 + i, step
            )

    def across(half, c):
        for which in (2, 3, 4, 5):
            copies[half, c, which].wait_recv()
        mine = h[half, c, at(half, False, 0)]
        g1[half, c] = (mine.astype(F32) + near1[half, c, 0].astype(F32) + near1[half, c, 1].astype(F32)).astype(BF16)
        for i, step in ((2, 2), (0, 1), (1, -1)):
            part = g1.at[half, c, pl.ds(pl.multiple_of(at(half, True, step) * 128, 128), 128)]
            copies[half, c, 6 + i] = ship(part, near2.at[half, c, i], True, half, c, 6 + i, step)

    def collect(half, c):
        total = g1[half, c, pl.ds(pl.multiple_of(at(half, True, 0) * 128, 128), 128)].astype(F32)
        for i in range(3):
            copies[half, c, 6 + i].wait_recv()
            total = total + near2[half, c, i].astype(F32)
        return total

    def z_target(k):
        far = jnp.where(k < 2, 16, 15 - (k - 2) // 4)
        sign = jnp.where(k < 2, 1, jnp.where(((k - 2) // 2) % 2 == 0, 1, -1))
        target = ((z + sign * far + 64) % 32) * 2 + (core + k) % 2
        return jnp.where(k == 62, z * 2 + (1 - core), target)

    def route(c, between=lambda: None):
        both = jnp.concatenate([collect(0, c), collect(1, c)], axis=1).astype(BF16)
        between()
        snd3[c] = mm(place[...], both, NT).reshape(64, 8, 128).astype(BF16)

        def send3(k, carry):
            t = z_target(k)
            pltpu.make_async_remote_copy(
                src_ref=snd3.at[c, t], dst_ref=r3.at[c, f], send_sem=z_send.at[c], recv_sem=z_recv.at[c], device_id=(s, t), device_id_type=MESH
            ).start()
            return carry

        lax.fori_loop(0, 63, send3, 0)
        r3[c, pl.ds(f, 1)] = snd3[c, pl.ds(f, 1)]

    halves = (0, 1)
    for half in halves:
        products(half, 0, 2)
        first_sends(half, 0, (0, 1))
    for half in halves:
        products(half, 0, 1)
        products(half, 0, -1)
        first_sends(half, 0, (2, 3))
    for half in halves:
        products(half, 0, 0)
        products(half, 1, 2)
        products(half, 1, 1)
        products(half, 1, -1)
    for half in halves:
        relayed_sends(half, 0)
    for half in halves:
        products(half, 1, 0)
    ques_row = jnp.sum(logit_all * projected, axis=0, keepdims=True)
    ques_ref[0] = (span_mask * ques_row / count).astype(BF16)

    def next_sends(whiches):
        for half in halves:
            first_sends(half, 1, whiches)

    for half in halves:
        across(half, 0)
    next_sends((0, 1))
    pl.semaphore_wait(z_near.at[3], 2)
    route(0, lambda: next_sends((2, 3)))
    for half in halves:
        relayed_sends(half, 1)
    for half in halves:
        across(half, 1)
    route(1)

    slots = out_ref.shape[2]
    row_id = lax.broadcasted_iota(jnp.int32, (rows, slots), 0)
    slot_id = lax.broadcasted_iota(jnp.int32, (rows, slots), 1)
    meets = (row_id >> 3) * 4 + (row_id & 3) == slot_id
    takes = [(meets & (((row_id >> 2) & 1) == half)).astype(F32).astype(BF16) for half in halves]
    for i, view in ((0, h.at[:, :, pl.ds(0, 3)]), (1, near2)):
        pltpu.make_async_copy(view, view, red_send.at[i]).wait()
    wait_all(r1, 15, ex_send, 0)
    wait_all(r2, 15, ex_send, 1)

    def wait_z(amount, c, sems):
        view = r3.at[c, pl.ds(0, amount)]
        pltpu.make_async_copy(view, view, sems.at[c]).wait()

    def finish(c):
        wait_z(63, c, z_recv)
        arrived = r3[c].astype(F32).reshape(rows, 128).astype(BF16)
        for half in halves:
            at_rows = slice(half * 256 + c * 128, half * 256 + c * 128 + 128)
            out_ref[0, at_rows] = (mm(arrived, takes[half], TN) * slope[at_rows]).astype(BF16)

    finish(0)
    for c in range(2):
        wait_z(63, c, z_send)
    finish(1)


def solution(mesh):
    def body(value_grad, w_value, norm_gain, vis_pos, frame_owner, ques_span, vis_proj, vis_resid, ques_hidden, w_down, pre_owned):
        model_width = vis_proj.shape[2] * mesh.shape["seq"]
        in_vmem = pl.BlockSpec(memory_space=pltpu.VMEM)
        in_hbm = pl.BlockSpec(memory_space=pltpu.HBM)
        dma = pltpu.SemaphoreType.DMA
        return pl.pallas_call(
            functools.partial(kernel, model_width),
            out_shape=(
                jax.ShapeDtypeStruct(pre_owned.shape, BF16),
                jax.ShapeDtypeStruct(ques_hidden.shape, BF16),
            ),
            in_specs=[in_hbm] * 11,
            out_specs=(in_vmem, in_vmem),
            scratch_shapes=[
                pltpu.VMEM((1024, 512), BF16),
                pltpu.VMEM((512, 512), BF16),
                pltpu.VMEM((1, 512), F32),
                pltpu.VMEM((1, 128), jnp.int32),
                pltpu.VMEM((1, 128), jnp.int32),
                pltpu.VMEM((1, 2), jnp.int32),
                pltpu.VMEM((128, 512), BF16),
                pltpu.VMEM((128, 512), BF16),
                pltpu.VMEM((32, 512), BF16),
                pltpu.VMEM((8192, 512), BF16),
                pltpu.VMEM((512, 256), BF16),
                pltpu.VMEM((16, 16, 640), BF16),
                pltpu.VMEM((16, 16, 640), BF16),
                pltpu.VMEM((8, 640), BF16),
                pltpu.VMEM((16, 8, 640), BF16),
                pltpu.VMEM((2, 2, 4, 512, 128), BF16),
                pltpu.VMEM((2, 2, 2, 256, 128), BF16),
                pltpu.VMEM((2, 2, 2, 256, 128), BF16),
                pltpu.VMEM((2, 2, 2, 512, 128), BF16),
                pltpu.VMEM((2, 2, 512, 128), BF16),
                pltpu.VMEM((2, 2, 3, 128, 128), BF16),
                pltpu.VMEM((512, 256), BF16),
                pltpu.VMEM((512, 256), F32),
                pltpu.VMEM((2, 64, 8, 128), BF16),
                pltpu.VMEM((2, 64, 8, 128), BF16),
                dma((11,)),
                dma((2,)),
                dma((2,)),
                dma((2,)),
                dma((2, 2, 9)),
                dma((2,)),
                dma((2,)),
                pltpu.SemaphoreType.REGULAR((4,)),
            ],
            compiler_params=pltpu.CompilerParams(collective_id=0, has_side_effects=True, vmem_limit_bytes=24 * 1024 * 1024),
        )(
            *(
                pltpu.with_memory_space_constraint(value, pltpu.HBM)
                for value in (
                    value_grad,
                    w_value,
                    norm_gain.reshape(1, -1),
                    vis_pos,
                    frame_owner.reshape(1, -1),
                    ques_span,
                    vis_proj,
                    vis_resid,
                    ques_hidden,
                    w_down,
                    pre_owned,
                )
            )
        )

    in_specs = (
        P("frame", "seq", None),
        P("seq", None),
        P("seq"),
        P("frame", None),
        P("frame", None, None),
        P("frame", None),
        P("frame", None, "seq"),
        P("frame", None, "seq"),
        P("frame", None, "seq"),
        P(None, "seq"),
        P("frame", "seq", None),
    )
    out_specs = (P("frame", "seq", None), P("frame", None, "seq"))
    return jax.shard_map(body, mesh=mesh, in_specs=in_specs, out_specs=out_specs, check_vma=False)
```
